512 devices in a mesh: shard: 128 (over z, x, core), rep: 4 (over y).
Axes of the slice: x: 4, y: 4, z: 16, core: 2. Of those that a mesh axis runs over, the one named last changes fastest.
Arguments:
- queries: bfloat16 [512, 32, 128], P(('rep', 'shard')), may hold values from -6 to 6
- passages: bfloat16 [512, 128, 128], P(('shard', 'rep')), may hold values from -0.52734375 to 0.52734375
- labels: int32 [512, 128], P('shard'), may hold values from 0 to 9
- lengths: int32 [512], P('shard'), may hold values from 16 to 128
- candidates: int32 [512, 256], P(('rep', 'shard')), may hold values from 0 to 511, all different within a row
- feedback: int32 [512, 3], P('rep'), may hold values from 0 to 511
- idf: int32 [512, 10], P('rep'), may hold values from 1 to 16
Outputs:
- first_scores: float32 [512, 256], P(('rep', 'shard'))
- final_scores: float32 [512, 256], P(('rep', 'shard'))
The draws below stay inside these ranges and needn't reach their ends.
Inputs may be any that keep to these rules, and one draw needn't show every extreme that they name: `candidates`: each row names 256 different passages; every passage is named by some row. `feedback`: ids may repeat within a row.
All inputs are finite; a program needn't handle non-finite values.
Results may differ from the reference program's by a relative error of at most 0.0003.
Values may be sent and summed in bfloat16 or wider, within the bound.
A program may use at most 64 MiB of HBM per device.

```python
import jax
import jax.numpy as jnp
from jax import lax

D = 128
QTOK = 32
PTOK = 128
NCLUS = 10
FB = 3
QUERIES = 512
PASSAGES = 512
NCAND = 256


def draw_lengths(key, part):
    drawn = jax.random.randint(key, (PASSAGES,), PTOK // 8, PTOK + 1, dtype=jnp.int32)
    drawn = drawn.at[0].set(PTOK)
    return drawn.at[1].set(PTOK // 8)


def set_ends(values, stream_key, low, high):
    spot = [jax.random.randint(jax.random.fold_in(stream_key, axis), (), 0, length) for axis, length in enumerate(values.shape)]
    widest = values.shape.index(max(values.shape))
    neighbour = spot[:widest] + [(spot[widest] + 1) % values.shape[widest]] + spot[widest + 1:]
    return values.at[tuple(spot)].set(low).at[tuple(neighbour)].set(high)


def block_levels(rng, shape, pieces, least, high):
    def one(dim, parts):
        steps = jax.random.uniform(jax.random.fold_in(jax.random.fold_in(rng, 6), dim), (parts,), jnp.float32, least / len(pieces), high / len(pieces))
        return jnp.repeat(jnp.exp(steps), shape[dim] // parts).reshape((-1,) + (1,) * (len(shape) - dim - 1))

    loudness = one(*pieces[0])
    for cut in pieces[1:]:
        loudness = loudness * one(*cut)
    return loudness


def choose_distinct(own_key, rows, amount, top, lift):
    ranking = jax.random.permutation(jax.random.fold_in(own_key, 1), amount)
    favour = ranking
    for power in range(3):
        favour = favour * favour // amount
    favour = favour * lift // amount
    chance = jax.random.randint(jax.random.fold_in(own_key, 2), (rows, amount), 0, 4096) + favour
    sure = jax.random.permutation(jax.random.fold_in(own_key, 3), rows)[jnp.arange(amount) % rows]
    chance = jnp.where(jnp.arange(rows)[:, None] == sure[None, :], 1 << 14, chance)
    merit = chance * amount + jnp.arange(amount)
    return lax.top_k(merit.astype(jnp.int32), top)[1].astype(jnp.int32)


def bell_draw(key, dims, spread, reach, cuts=(), kind=jnp.bfloat16):
    result = jax.random.normal(key, dims, jnp.float32) * spread
    if len(cuts) > 0:
        result = block_levels(key, dims, cuts, -0.22, 0.18) * result
    return jnp.clip(result, min=-reach, max=reach).astype(kind)


def setup_inputs(seed: int = 0) -> dict:
    seeds = jax.random.split(jax.random.key(seed), 8)
    queries = bell_draw(seeds[0], (QUERIES, QTOK, D), 1.0, 6.0, ((0, 512),))
    passages = bell_draw(seeds[1], (PASSAGES, PTOK, D), 0.0884, 0.52734375, ((0, 512),))
    labels = set_ends(jax.random.randint(seeds[2], (PASSAGES, PTOK), 0, NCLUS), jax.random.fold_in(seeds[2], 1), 0, NCLUS - 1).astype(jnp.int32)
    lengths = draw_lengths(jax.random.fold_in(seeds[7], 71), 0)
    candidates = choose_distinct(seeds[4], QUERIES, PASSAGES, NCAND, 8192)
    feedback = set_ends(jax.random.randint(seeds[5], (QUERIES, FB), 0, PASSAGES), jax.random.fold_in(seeds[5], 1), 0, PASSAGES - 1).astype(jnp.int32)
    idf = set_ends(jax.random.randint(seeds[6], (QUERIES, NCLUS), 1, 17), jax.random.fold_in(seeds[6], 1), 1, 16).astype(jnp.int32)
    return {"queries": queries, "passages": passages, "labels": labels, "lengths": lengths, "candidates": candidates, "feedback": feedback, "idf": idf}


def cluster_totals(passages, labels, lengths):
    positions = jnp.arange(PTOK, dtype=jnp.int32)
    in_length = positions[None, :] < lengths[:, None]
    clusters = jnp.arange(NCLUS, dtype=jnp.int32)
    one_hot = ((labels[:, :, None] == clusters[None, None, :]) & in_length[:, :, None]).astype(jnp.float32)
    return jnp.einsum('ptc,ptd->pcd', one_hot, passages.astype(jnp.float32), precision=lax.Precision.HIGHEST)

def normalize(pooled):
    factor = lax.rsqrt(lax.optimization_barrier(jnp.mean(pooled * pooled, axis=-1, keepdims=True)) + 1e-06)
    return (pooled * factor).astype(jnp.bfloat16)

def reference(queries, passages, labels, lengths, candidates, feedback, idf):
    totals = cluster_totals(passages, labels, lengths)
    pooled = lax.optimization_barrier(jnp.sum(jnp.take(totals, feedback, axis=0), axis=1))
    expansion = normalize(pooled)
    weights = idf.astype(jnp.float32) / (8.0 * NCLUS)
    positions = jnp.arange(PTOK, dtype=jnp.int32)

    def one_query(operand):
        query_vectors, expanded_rows, weight_row, candidate_ids = operand
        documents = jnp.take(passages, candidate_ids, axis=0).astype(jnp.float32)
        in_length = positions[None, :] < jnp.take(lengths, candidate_ids, axis=0)[:, None]
        combined = jnp.concatenate([query_vectors, expanded_rows], axis=0).astype(jnp.float32)
        scores = jnp.einsum('id,ktd->kit', combined, documents, precision=lax.Precision.HIGHEST)
        best_scores = lax.optimization_barrier(jnp.max(jnp.where(in_length[:, None, :], scores, -1000000000.0), axis=-1))
        plain_score = lax.optimization_barrier(jnp.mean(best_scores[:, :QTOK], axis=1))
        added_score = lax.optimization_barrier(jnp.sum(best_scores[:, QTOK:] * weight_row[None, :], axis=1))
        return (plain_score, plain_score + added_score)
    first_scores, final_scores = lax.map(one_query, (queries, expansion, weights, candidates))
    return (first_scores, final_scores)
```

```python
import functools

import jax
import jax.numpy as jnp
from jax import lax
from jax.experimental import pallas as pl
from jax.experimental.pallas import tpu as pltpu
from jax.sharding import PartitionSpec as P

MESH = pl.DeviceIdType.MESH
F32 = jnp.float32
BF16 = jnp.bfloat16
NT = (((1,), (1,)), ((), ()))

NZ, NX, NY, NC = 16, 4, 4, 2
PLANE = NX * NY * NC
ROW = NX * NC
QTOK, PTOK, D = 32, 128, 128
NCLUS, CPAD, FB = 10, 16, 3
NCAND = 256
WIDE = NCLUS * D
QROWS = PLANE * QTOK
EROWS = PLANE * CPAD
CHUNKS = 2
TILE = 256
RS_ORDER = (8, 7, 9, 6, 10, 5, 11, 4, 12, 3, 13, 2, 14, 1, 15)
RELAYS = (
    (0, ((2, 2), (-2, 14), (1, 1), (-1, 15))),
    (2, ((2, 4), (1, 3))),
    (14, ((-2, 12), (-1, 13))),
    (4, ((2, 6), (1, 5))),
    (12, ((-2, 10), (-1, 11))),
    (6, ((2, 8), (1, 7))),
    (10, ((-1, 9),)),
)


def ring(n):
    return min(n, 4 - n)


OFFSETS = sorted(
    [(dy, dx, dc) for dy in range(NY) for dx in range(NX) for dc in range(NC)][1:],
    key=lambda o: -(ring(o[0]) + ring(o[1])),
)


def iota(shape, dim):
    return lax.broadcasted_iota(jnp.int32, shape, dim)


def split3(a):
    hi = a.astype(BF16)
    rest = a - hi.astype(F32)
    mid = rest.astype(BF16)
    low = (rest - mid.astype(F32)).astype(BF16)
    return hi, mid, low


def kernel(
    q_hbm, p_hbm, lab_hbm, len_ref, cand_hbm, fb_hbm, idf_hbm,
    first_ref, final_ref,
    qbuf, praw, pas, lab, cand, fb, idf, tot, part, rs, es, exb, best, back, ret,
    load_sem, tot_send, tot_recv, query_send, query_recv, pas_send, pas_recv,
    rs_send, rs_recv, exp_send, exp_recv, ret_send, ret_recv, near_sem, far_sem,
):
    s = lax.axis_index("shard")
    y = lax.axis_index("rep")
    core = lax.rem(s, 2)
    x = lax.rem(lax.div(s, 2), NX)
    z = lax.div(s, ROW)

    def device(dz=0, dy=0, dx=0, dc=0):
        tz = lax.rem(z + (dz + NZ), NZ)
        ty = lax.rem(y + (dy + NY), NY)
        tx = lax.rem(x + (dx + NX), NX)
        tc = lax.rem(core + dc, 2)
        return ((tz * NX + tx) * NC + tc, ty)

    def remote(src, dst, send, recv, to):
        return pltpu.make_async_remote_copy(
            src_ref=src, dst_ref=dst, send_sem=send, recv_sem=recv, device_id=to, device_id_type=MESH
        )

    row_steps = [(dx, dc) for dx in (2, 1, 3, 0) for dc in (0, 1) if (dx, dc) != (0, 0)]
    barrier = pltpu.get_barrier_semaphore()
    near = [device(dx=dx, dc=dc) for dx, dc in row_steps]
    near += [device(dy=dy) for dy in (2, 1, 3)]
    near += [device(dz=dz) for dz in (2, -2, 1, -1)]
    for to in near:
        pl.semaphore_signal(barrier, inc=1, device_id=to, device_id_type=MESH)

    loads = [
        pltpu.make_async_copy(src, dst, load_sem.at[i])
        for i, (src, dst) in enumerate(
            (
                (p_hbm.at[0], praw),
                (lab_hbm, lab),
                (q_hbm.at[0], qbuf.at[0, 0]),
                (idf_hbm, idf),
                (fb_hbm, fb),
                (cand_hbm, cand),
            )
        )
    ]
    for copy in loads:
        copy.start()

    length = len_ref[y]
    loads[0].wait()
    loads[1].wait()
    passage = praw[...]
    labels = lab[pl.ds(y, 1), :]
    picked = (iota((CPAD, PTOK), 0) == labels) & (iota((CPAD, PTOK), 1) < length)
    totals = jnp.dot(
        jnp.where(picked, 1.0, 0.0).astype(BF16), passage, preferred_element_type=F32
    )
    for c in range(NCLUS):
        tot[0, 0:1, c * D : (c + 1) * D] = totals[c : c + 1, :]
    wide = passage.astype(F32)
    masked = jnp.where(iota((PTOK, D), 0) < length, wide, wide[0:1, :])
    pas[0] = masked.astype(BF16)
    loads[2].wait()
    loads[3].wait()
    tot[0, 0:1, WIDE : WIDE + D] = jnp.zeros((1, D), F32)
    mine = jnp.where(iota((8, NZ * ROW), 1) == s, 1.0, 0.0).astype(BF16)
    weights = lax.dot_general(mine, idf[...].astype(F32).astype(BF16), NT, preferred_element_type=F32)
    tot[0, 0:1, WIDE : WIDE + NCLUS] = weights[0:1, :]
    back[...] = jnp.zeros_like(back)

    pl.semaphore_wait(barrier, len(near))

    sends = []

    def go(copy):
        copy.start()
        sends.append(copy)

    for dz in (2, -2):
        pl.semaphore_signal(near_sem, inc=1, device_id=device(dz=dz), device_id_type=MESH)

    def pass_copy(source, slot, dz, chunk):
        rows = pl.ds(chunk * (PTOK // CHUNKS), PTOK // CHUNKS)
        k = slot * CHUNKS + chunk
        return remote(
            pas.at[source, rows], pas.at[slot, rows], pas_send.at[k], pas_recv.at[k], device(dz=dz)
        )

    def pass_wait(slot, chunk):
        pass_copy(slot, slot, 1, chunk).wait_recv()

    def relay(entry):
        source, hops = entry
        for chunk in range(CHUNKS):
            if source:
                pass_wait(source, chunk)
            for dz, slot in hops:
                go(pass_copy(source, slot, dz, chunk))

    row_tot, row_query = [], []
    for dx, dc in row_steps:
        slot = dx * NC + dc
        copy = remote(
            tot.at[0, pl.ds(0, 1)], tot.at[0, pl.ds(slot, 1)],
            tot_send.at[slot], tot_recv.at[slot], device(dx=dx, dc=dc),
        )
        go(copy)
        row_tot.append(copy)
    relay(RELAYS[0])
    for dx, dc in row_steps:
        slot = dx * NC + dc
        copy = remote(
            qbuf.at[0, 0], qbuf.at[0, slot],
            query_send.at[slot], query_recv.at[slot], device(dx=dx, dc=dc),
        )
        go(copy)
        row_query.append(copy)

    loads[4].wait()
    loads[5].wait()
    turn = lax.rem(iota((NZ, NZ * ROW), 0) + z, NZ) * ROW + (x * NC + core)
    pick = jnp.where(iota((NZ, NZ * ROW), 1) == turn, 1.0, 0.0).astype(F32)
    ids = lax.dot_general(
        pick, fb[...].astype(F32), NT,
        precision=lax.Precision.HIGHEST, preferred_element_type=F32,
    )
    slots = iota((NZ, PLANE), 1)
    slot_y = lax.rem(y + NY - lax.div(slots, ROW), NY)
    slot_x = lax.rem(x + NX - lax.rem(lax.div(slots, NC), NX), NX)
    slot_c = lax.rem(core + lax.rem(slots, NC), 2)
    slot_id = (z * PLANE + slot_x * (NC * NY) + slot_c * NY + slot_y).astype(F32)
    counts = jnp.zeros((NZ, PLANE), F32)
    for k in range(FB):
        counts += jnp.where(jnp.abs(slot_id - ids[:, k : k + 1]) < 0.5, 1.0, 0.0)
    counts = counts.astype(BF16)

    for copy in row_tot:
        copy.wait_recv()
    col_tot, col_query = [], []
    for dy in (2, 1, 3):
        copy = remote(
            tot.at[0], tot.at[dy], tot_send.at[ROW + dy], tot_recv.at[ROW + dy], device(dy=dy)
        )
        go(copy)
        col_tot.append(copy)
    pl.semaphore_wait(near_sem, 2)
    for dz in (4, -4):
        pl.semaphore_signal(far_sem, inc=1, device_id=device(dz=dz), device_id_type=MESH)
    for copy in row_query:
        copy.wait_recv()
    for dy in (2, 1, 3):
        copy = remote(
            qbuf.at[0], qbuf.at[dy],
            query_send.at[ROW + dy], query_recv.at[ROW + dy], device(dy=dy),
        )
        go(copy)
        col_query.append(copy)
    relay(RELAYS[1])
    relay(RELAYS[2])
    for copy in col_tot:
        copy.wait_recv()

    table = tot[...].reshape(PLANE, WIDE + D)
    summed = None
    for piece in split3(table[:, :WIDE]):
        term = jnp.dot(counts, piece, preferred_element_type=F32)
        summed = term if summed is None else summed + term
    part[...] = summed
    pl.semaphore_wait(far_sem, 2)
    parts = []
    for dz in RS_ORDER:
        copy = remote(
            part.at[pl.ds(dz, 1)], rs.at[pl.ds(dz, 1)],
            rs_send.at[dz], rs_recv.at[dz], device(dz=dz),
        )
        go(copy)
        parts.append(copy)
    rs[0:1, :] = summed[0:1, :]

    owner = lax.div(iota((PLANE, EROWS), 1), CPAD)
    spread = jnp.where(
        lax.rem(iota((D, EROWS), 1), CPAD) == iota((D, EROWS), 0), 1.0, 0.0
    ).astype(BF16)
    idf_rows = jnp.dot(table[:, WIDE:].astype(BF16), spread, preferred_element_type=F32)
    exp_weight = jnp.where(owner == iota((PLANE, EROWS), 0), idf_rows, 0.0).astype(BF16)
    query_weight = jnp.where(
        lax.div(iota((PLANE, QROWS), 1), QTOK) == iota((PLANE, QROWS), 0), 1.0, 0.0
    ).astype(BF16)

    for entry in RELAYS[3:]:
        relay(entry)

    for copy in parts:
        copy.wait_recv()
    pooled = jnp.sum(rs[...], axis=0, keepdims=True)
    es[...] = jnp.zeros_like(es)
    for c in range(NCLUS):
        es[c : c + 1, :] = pooled[:, c * D : (c + 1) * D]
    rows = es[...]
    factor = lax.rsqrt(jnp.mean(rows * rows, axis=1, keepdims=True) + 1e-06)
    exb[0] = (rows * factor).astype(BF16)
    expansions = []
    for dy, dx, dc in OFFSETS:
        slot = dy * ROW + dx * NC + dc
        copy = remote(
            exb.at[0], exb.at[slot], exp_send.at[slot], exp_recv.at[slot],
            device(dy=dy, dx=dx, dc=dc),
        )
        go(copy)
        expansions.append(copy)

    for copy in col_query:
        copy.wait_recv()
    for slot in (1, 15, 3, 13, 5, 11, 7, 9, 8):
        for chunk in range(CHUNKS):
            pass_wait(slot, chunk)

    def maxima(vectors, n):
        scores = lax.dot_general(pas[n], vectors, NT, preferred_element_type=F32)
        return jnp.max(scores, axis=0, keepdims=True)

    for tile in range(QROWS // TILE):
        vectors = qbuf[tile // 1].reshape(ROW * QTOK, D)
        for n in range(NZ):
            best[n : n + 1, tile * TILE : (tile + 1) * TILE] = maxima(vectors, n)

    def reduce(weight, values):
        hi, mid, low = split3(values)
        total = lax.dot_general(weight, hi, NT, preferred_element_type=F32)
        total += lax.dot_general(weight, mid, NT, preferred_element_type=F32)
        return total + lax.dot_general(weight, low, NT, preferred_element_type=F32)

    plain = reduce(query_weight, best[:, :QROWS]) * (1.0 / QTOK)
    back[:, 0:NZ] = plain

    ids = cand[...]
    cand_y = lax.rem(ids, NY)
    cand_c = lax.rem(lax.div(ids, NY), NC)
    cand_x = lax.rem(lax.div(ids, NY * NC), NX)
    cand_z = lax.div(ids, PLANE)
    cand_slot = (
        lax.rem(cand_y + NY - y, NY) * ROW
        + lax.rem(cand_x + NX - x, NX) * NC
        + lax.rem(cand_c + core, 2)
    )
    cand_n = lax.rem(z + NZ - cand_z, NZ)
    slot_hot = jnp.where(iota((PLANE, NCAND), 0) == cand_slot, 1.0, 0.0).astype(BF16)
    n_hot = iota((NZ, NCAND), 0) == cand_n

    for copy in expansions:
        copy.wait_recv()
    for tile in range(EROWS // TILE):
        part_rows = TILE // CPAD
        vectors = exb[tile * part_rows : (tile + 1) * part_rows].reshape(TILE, D)
        for n in range(NZ):
            at = QROWS + tile * TILE
            best[n : n + 1, at : at + TILE] = maxima(vectors, n)
    added = reduce(exp_weight, best[:, QROWS:]) * (1.0 / (8.0 * NCLUS))
    back[:, NZ : 2 * NZ] = plain + added

    returns = []
    for dy, dx, dc in OFFSETS:
        slot = dy * ROW + dx * NC + dc
        copy = remote(
            back.at[pl.ds(slot, 1)], ret.at[pl.ds(slot, 1)],
            ret_send.at[slot], ret_recv.at[slot], device(dy=-dy, dx=-dx, dc=dc),
        )
        go(copy)
        returns.append(copy)
    ret[0:1, :] = back[0:1, :]
    for copy in returns:
        copy.wait_recv()
    flat = ret[...].T[: 2 * NZ, :]
    chosen = None
    for piece in split3(flat):
        term = jnp.dot(piece, slot_hot, preferred_element_type=F32)
        chosen = term if chosen is None else chosen + term
    first_ref[...] = jnp.sum(jnp.where(n_hot, chosen[:NZ], 0.0), axis=0, keepdims=True)
    final_ref[...] = jnp.sum(jnp.where(n_hot, chosen[NZ:], 0.0), axis=0, keepdims=True)
    for copy in sends:
        copy.wait_send()


def local(queries, passages, labels, lengths, candidates, feedback, idf):
    dma = pltpu.SemaphoreType.DMA
    anywhere = pl.BlockSpec(memory_space=pl.ANY)
    return pl.pallas_call(
        kernel,
        out_shape=(
            jax.ShapeDtypeStruct((1, NCAND), F32),
            jax.ShapeDtypeStruct((1, NCAND), F32),
        ),
        in_specs=[anywhere] * 3 + [pl.BlockSpec(memory_space=pltpu.SMEM)] + [anywhere] * 3,
        out_specs=(
            pl.BlockSpec(memory_space=pltpu.VMEM),
            pl.BlockSpec(memory_space=pltpu.VMEM),
        ),
        scratch_shapes=[
            pltpu.VMEM((NY, ROW, QTOK, D), BF16),
            pltpu.VMEM((PTOK, D), BF16),
            pltpu.VMEM((NZ, PTOK, D), BF16),
            pltpu.VMEM((NY, PTOK), jnp.int32),
            pltpu.VMEM((1, NCAND), jnp.int32),
            pltpu.VMEM((FB, NZ * ROW), jnp.int32),
            pltpu.VMEM((NCLUS, NZ * ROW), jnp.int32),
            pltpu.VMEM((NY, ROW, WIDE + D), F32),
            pltpu.VMEM((NZ, WIDE), F32),
            pltpu.VMEM((NZ, WIDE), F32),
            pltpu.VMEM((CPAD, D), F32),
            pltpu.VMEM((PLANE, CPAD, D), BF16),
            pltpu.VMEM((NZ, QROWS + EROWS), F32),
            pltpu.VMEM((PLANE, D), F32),
            pltpu.VMEM((PLANE, D), F32),
            dma((6,)),
            dma((ROW + NY,)), dma((ROW + NY,)),
            dma((ROW + NY,)), dma((ROW + NY,)),
            dma((NZ * CHUNKS,)), dma((NZ * CHUNKS,)),
            dma((NZ,)), dma((NZ,)),
            dma((PLANE,)), dma((PLANE,)),
            dma((PLANE,)), dma((PLANE,)),
            pltpu.SemaphoreType.REGULAR,
            pltpu.SemaphoreType.REGULAR,
        ],
        compiler_params=pltpu.CompilerParams(collective_id=0, has_side_effects=True),
    )(queries, passages, labels, lengths, candidates, feedback.T, idf.T)


def solution(mesh):
    return jax.shard_map(
        local,
        mesh=mesh,
        in_specs=(
            P(("rep", "shard"), None, None),
            P(("shard", "rep"), None, None),
            P("shard", None),
            P("shard"),
            P(("rep", "shard"), None),
            P("rep", None),
            P("rep", None),
        ),
        out_specs=(P(("rep", "shard"), None), P(("rep", "shard"), None)),
        check_vma=False,
    )
```

```python
import functools

import jax
import jax.numpy as jnp
from jax import lax
from jax.experimental import pallas as pl
from jax.experimental.pallas import tpu as pltpu
from jax.sharding import PartitionSpec as P

MESH = pl.DeviceIdType.MESH
F32 = jnp.float32
BF16 = jnp.bfloat16
NT = (((1,), (1,)), ((), ()))

NZ, NX, NY, NC = 16, 4, 4, 2
PLANE = NX * NY * NC
ROW = NX * NC
QTOK, PTOK, D = 32, 128, 128
NCLUS, CPAD, FB = 10, 16, 3
NCAND = 256
QROWS = PLANE * QTOK
EROWS = PLANE * CPAD
EXP = NZ * CPAD
CHUNKS = 2
TILE = 256
RS_ORDER = (8, 7, 9, 6, 10, 5, 11, 4, 12, 3, 13, 2, 14, 1, 15)
RELAYS = (
    (0, ((2, 2), (-2, 14), (1, 1), (-1, 15))),
    (2, ((2, 4), (1, 3))),
    (14, ((-2, 12), (-1, 13))),
    (4, ((2, 6), (1, 5))),
    (12, ((-2, 10), (-1, 11))),
    (6, ((2, 8), (1, 7))),
    (10, ((-1, 9),)),
)


def ring(n):
    return min(n, 4 - n)


OFFSETS = sorted(
    [(dy, dx, dc) for dy in range(NY) for dx in range(NX) for dc in range(NC)][1:],
    key=lambda o: -(ring(o[0]) + ring(o[1])),
)


def iota(shape, dim):
    return lax.broadcasted_iota(jnp.int32, shape, dim)


def split3(a):
    hi = a.astype(BF16)
    rest = a - hi.astype(F32)
    mid = rest.astype(BF16)
    low = (rest - mid.astype(F32)).astype(BF16)
    return hi, mid, low


def kernel(
    q_hbm, p_hbm, lab_hbm, len_hbm, cand_hbm, fb_hbm, idf_hbm,
    out_ref,
    len_ref, qbuf, praw, pas, lab, cand, fb, idf, tot, mix, part, rs, exb, best, back, ret,
    load_sem, tot_send, row_tot_recv, col_tot_recv, query_send, row_query_recv, col_query_recv,
    pas_send, relay_recv, odd_recv, end_recv, rs_send, rs_recv, exp_send, exp_recv, ret_send, ret_recv, near_sem, far_sem,
):
    s = lax.axis_index("shard")
    y = lax.axis_index("rep")
    core = lax.rem(s, 2)
    x = lax.rem(lax.div(s, 2), NX)
    z = lax.div(s, ROW)

    def device(dz=0, dy=0, dx=0, dc=0):
        tz = lax.rem(z + (dz + NZ), NZ)
        ty = lax.rem(y + (dy + NY), NY)
        tx = lax.rem(x + (dx + NX), NX)
        tc = lax.rem(core + dc, 2)
        return ((tz * NX + tx) * NC + tc, ty)

    def remote(src, dst, send, recv, to):
        return pltpu.make_async_remote_copy(
            src_ref=src, dst_ref=dst, send_sem=send, recv_sem=recv, device_id=to, device_id_type=MESH
        )

    row_steps = [(0, 1), (1, 0), (3, 0), (1, 1), (3, 1), (2, 0), (2, 1)]
    barrier = pltpu.get_barrier_semaphore()
    near = [device(dx=dx, dc=dc) for dx, dc in row_steps]
    near += [device(dy=dy) for dy in (2, 1, 3)]
    near += [device(dz=dz) for dz in (2, -2, 1, -1)]
    for to in near:
        pl.semaphore_signal(barrier, inc=1, device_id=to, device_id_type=MESH)

    loads = [
        pltpu.make_async_copy(src, dst, load_sem.at[i])
        for i, (src, dst) in enumerate(
            (
                (p_hbm.at[0], praw),
                (lab_hbm, lab),
                (q_hbm.at[0], qbuf.at[0]),
                (idf_hbm, idf),
                (fb_hbm, fb),
                (cand_hbm, cand),
                (len_hbm, len_ref),
            )
        )
    ]
    for copy in loads:
        copy.start()

    loads[6].wait()
    length = len_ref[y]
    loads[1].wait()
    loads[0].wait()
    passage = praw[...]
    labels = lab[pl.ds(y, 1), :]
    picked = (iota((CPAD, PTOK), 0) == labels) & (iota((CPAD, PTOK), 1) < length)
    totals = jnp.dot(
        jnp.where(picked, 1.0, 0.0).astype(BF16), passage, preferred_element_type=F32
    )
    wide = passage.astype(F32)
    masked = jnp.where(iota((PTOK, D), 0) < length, wide, wide[0:1, :])
    pas[0] = masked.astype(BF16)
    loads[2].wait()
    loads[3].wait()
    mine = jnp.where(
        (iota((CPAD, NZ * ROW), 1) == s) & (iota((CPAD, NZ * ROW), 0) == NCLUS), 1.0, 0.0
    ).astype(BF16)
    spread = jnp.where(
        iota((NCLUS, D), 0) == iota((NCLUS, D), 1), 1.0, 0.0
    ).astype(BF16)
    table = lax.dot_general(
        idf[...].astype(F32).astype(BF16), spread, (((0,), (0,)), ((), ())),
        preferred_element_type=F32,
    ).astype(BF16)
    tot[0] = totals + jnp.dot(mine, table, preferred_element_type=F32)
    back[...] = jnp.zeros_like(back)
    exb[...] = jnp.zeros_like(exb)

    pl.semaphore_wait(barrier, len(near))

    def arrive(ref, sem):
        remote(ref, ref, sem, sem, device(dc=1)).wait_recv()

    def leave(ref, sem):
        remote(ref, ref, sem, sem, device(dc=1)).wait_send()

    for dz in (2, -2):
        pl.semaphore_signal(near_sem, inc=1, device_id=device(dz=dz), device_id_type=MESH)

    def place(slot):
        return slot // 2 + (slot % 2) * (NZ // 2)

    def pass_rows(slot, chunk):
        return pas.at[place(slot), pl.ds(chunk * (PTOK // CHUNKS), PTOK // CHUNKS)]

    def pass_recv(slot, chunk):
        if slot % 2:
            return odd_recv
        return end_recv if slot == NZ // 2 else relay_recv.at[place(slot) * CHUNKS + chunk]

    def relay(entry):
        source, hops = entry
        for chunk in range(CHUNKS):
            if source:
                arrive(pass_rows(source, chunk), pass_recv(source, chunk))
            for dz, slot in hops:
                remote(
                    pass_rows(source, chunk), pass_rows(slot, chunk),
                    pas_send, pass_recv(slot, chunk), device(dz=dz),
                ).start()

    sent = pl.ds(0, NCLUS + 1)
    for dx, dc in row_steps:
        slot = dx * NC + dc
        remote(
            tot.at[0, sent], tot.at[slot, sent], tot_send, row_tot_recv.at[slot], device(dx=dx, dc=dc)
        ).start()

    def col_send(slot):
        for dy in (2, 1, 3):
            remote(
                tot.at[slot, sent], tot.at[dy * ROW + slot, sent],
                tot_send, col_tot_recv, device(dy=dy),
            ).start()

    col_send(0)
    relay(RELAYS[0])
    loads[4].wait()
    loads[5].wait()
    turn = lax.rem(iota((NZ, NZ * ROW), 0) + z, NZ) * ROW + (x * NC + core)
    pick = jnp.where(iota((NZ, NZ * ROW), 1) == turn, 1.0, 0.0).astype(F32)
    ids = lax.dot_general(
        pick, fb[...].astype(F32), NT,
        precision=lax.Precision.HIGHEST, preferred_element_type=F32,
    )
    slots = iota((NZ, PLANE), 1)
    slot_y = lax.rem(y + NY - lax.div(slots, ROW), NY)
    slot_x = lax.rem(x + NX - lax.rem(lax.div(slots, NC), NX), NX)
    slot_c = lax.rem(core + lax.rem(slots, NC), 2)
    slot_id = (z * PLANE + slot_x * (NC * NY) + slot_c * NY + slot_y).astype(F32)
    counts = jnp.zeros((NZ, PLANE), F32)
    for k in range(FB):
        counts += jnp.where(jnp.abs(slot_id - ids[:, k : k + 1]) < 0.5, 1.0, 0.0)
    up = jnp.where(lax.div(iota((EXP, NZ), 0), CPAD) == iota((EXP, NZ), 1), 1.0, 0.0).astype(BF16)
    over = jnp.where(
        lax.div(iota((PLANE, EROWS), 1), CPAD) == iota((PLANE, EROWS), 0), 1.0, 0.0
    ).astype(BF16)
    tall = jnp.dot(up, counts.astype(BF16), preferred_element_type=F32).astype(BF16)
    counts = jnp.dot(tall, over, preferred_element_type=F32)
    same = lax.rem(iota((EXP, EROWS), 0), CPAD) == lax.rem(iota((EXP, EROWS), 1), CPAD)
    mix[...] = jnp.where(same, counts, 0.0).astype(BF16)

    for dx, dc in row_steps:
        slot = dx * NC + dc
        arrive(tot.at[slot, sent], row_tot_recv.at[slot])
        col_send(slot)
    for dx, dc in row_steps:
        slot = dx * NC + dc
        remote(
            qbuf.at[0], qbuf.at[slot], query_send, row_query_recv, device(dx=dx, dc=dc)
        ).start()
    pl.semaphore_wait(near_sem, 2)
    for dz in (4, -4):
        pl.semaphore_signal(far_sem, inc=1, device_id=device(dz=dz), device_id_type=MESH)
    relay(RELAYS[1])
    relay(RELAYS[2])
    arrive(tot.at[pl.ds(ROW, PLANE - ROW), sent], col_tot_recv)

    table = jnp.where(iota((PLANE, CPAD, D), 1) < NCLUS, tot[...], 0.0).reshape(EROWS, D)
    counts = mix[...]
    summed = None
    for piece in split3(table):
        term = jnp.dot(counts, piece, preferred_element_type=F32)
        summed = term if summed is None else summed + term
    part[...] = summed.reshape(NZ, CPAD, D)
    pl.semaphore_wait(far_sem, 2)
    for dz in RS_ORDER:
        remote(
            part.at[dz, pl.ds(0, NCLUS)], rs.at[dz, pl.ds(0, NCLUS)],
            rs_send, rs_recv, device(dz=dz),
        ).start()
    arrive(qbuf.at[pl.ds(1, ROW - 1)], row_query_recv)
    for dy in (2, 1, 3):
        remote(
            qbuf.at[pl.ds(0, ROW)], qbuf.at[pl.ds(dy * ROW, ROW)],
            query_send, col_query_recv, device(dy=dy),
        ).start()

    owner = lax.div(iota((PLANE, EROWS), 1), CPAD)
    spread = jnp.where(
        lax.rem(iota((D, EROWS), 1), CPAD) == iota((D, EROWS), 0), 1.0, 0.0
    ).astype(BF16)
    idf_rows = tot[:, NCLUS].astype(BF16)
    idf_rows = jnp.dot(idf_rows, spread, preferred_element_type=F32)
    exp_weight = jnp.where(owner == iota((PLANE, EROWS), 0), idf_rows, 0.0).astype(BF16)
    query_weight = jnp.where(
        lax.div(iota((PLANE, QROWS), 1), QTOK) == iota((PLANE, QROWS), 0), 1.0, 0.0
    ).astype(BF16)

    for entry in RELAYS[3:]:
        relay(entry)

    arrive(rs.at[pl.ds(1, NZ - 1), pl.ds(0, NCLUS)], rs_recv)
    rows = part[0, 0:NCLUS]
    for dz in range(1, NZ):
        rows += rs[dz, 0:NCLUS]
    factor = lax.rsqrt(jnp.mean(rows * rows, axis=1, keepdims=True) + 1e-06)
    exb[0, 0:NCLUS] = (rows * factor).astype(BF16)
    for dy, dx, dc in OFFSETS:
        slot = dy * ROW + dx * NC + dc
        remote(
            exb.at[0, pl.ds(0, NCLUS)], exb.at[slot, pl.ds(0, NCLUS)], exp_send, exp_recv,
            device(dy=dy, dx=dx, dc=dc),
        ).start()

    arrive(qbuf.at[pl.ds(ROW, PLANE - ROW)], col_query_recv)
    arrive(pas.at[pl.ds(NZ // 2, NZ // 2)], odd_recv)
    arrive(pas.at[NZ // 4], end_recv)

    def maxima(vectors, n):
        scores = lax.dot_general(pas[n], vectors, NT, preferred_element_type=F32)
        return jnp.max(scores, axis=0, keepdims=True)

    for tile in range(QROWS // TILE):
        vectors = qbuf[tile * ROW : (tile + 1) * ROW].reshape(TILE, D)
        for n in range(NZ):
            best[n : n + 1, tile * TILE : (tile + 1) * TILE] = maxima(vectors, n)

    def reduce(weight, values):
        hi, mid, low = split3(values)
        total = lax.dot_general(weight, hi, NT, preferred_element_type=F32)
        total += lax.dot_general(weight, mid, NT, preferred_element_type=F32)
        return total + lax.dot_general(weight, low, NT, preferred_element_type=F32)

    plain = reduce(query_weight, best[:, :QROWS]) * (1.0 / QTOK)
    back[:, 0:NZ] = plain

    ids = cand[...]
    cand_y = lax.rem(ids, NY)
    cand_c = lax.rem(lax.div(ids, NY), NC)
    cand_x = lax.rem(lax.div(ids, NY * NC), NX)
    cand_z = lax.div(ids, PLANE)
    cand_slot = (
        lax.rem(cand_y + NY - y, NY) * ROW
        + lax.rem(cand_x + NX - x, NX) * NC
        + lax.rem(cand_c + core, 2)
    )
    cand_n = lax.rem(z + NZ - cand_z, NZ)
    cand_n = lax.div(cand_n, 2) + lax.rem(cand_n, 2) * (NZ // 2)
    slot_hot = jnp.where(iota((PLANE, NCAND), 0) == cand_slot, 1.0, 0.0).astype(BF16)
    n_hot = iota((NZ, NCAND), 0) == cand_n

    arrive(exb.at[pl.ds(1, PLANE - 1), pl.ds(0, NCLUS)], exp_recv)
    for tile in range(EROWS // TILE):
        part_rows = TILE // CPAD
        vectors = exb[tile * part_rows : (tile + 1) * part_rows].reshape(TILE, D)
        for n in range(NZ):
            at = QROWS + tile * TILE
            best[n : n + 1, at : at + TILE] = maxima(vectors, n)
    added = reduce(exp_weight, best[:, QROWS:]) * (1.0 / (8.0 * NCLUS))
    back[:, NZ : 2 * NZ] = plain + added

    for dy, dx, dc in OFFSETS:
        slot = dy * ROW + dx * NC + dc
        remote(
            back.at[pl.ds(slot, 1)], ret.at[pl.ds(slot, 1)], ret_send, ret_recv,
            device(dy=-dy, dx=-dx, dc=dc),
        ).start()
    ret[0:1, :] = back[0:1, :]
    others = pl.ds(1, PLANE - 1)
    leave(tot.at[others, sent], tot_send)
    leave(qbuf.at[others], query_send)
    leave(pas.at[pl.ds(1, NZ - 1)], pas_send)
    leave(rs.at[pl.ds(1, NZ - 1), pl.ds(0, NCLUS)], rs_send)
    leave(exb.at[others, pl.ds(0, NCLUS)], exp_send)
    arrive(ret.at[others], ret_recv)
    flat = ret[...].T[: 2 * NZ, :]
    chosen = None
    for piece in split3(flat):
        term = jnp.dot(piece, slot_hot, preferred_element_type=F32)
        chosen = term if chosen is None else chosen + term
    out_ref[0:1, :] = jnp.sum(jnp.where(n_hot, chosen[:NZ], 0.0), axis=0, keepdims=True)
    out_ref[1:2, :] = jnp.sum(jnp.where(n_hot, chosen[NZ:], 0.0), axis=0, keepdims=True)
    leave(ret.at[others], ret_send)


def local(queries, passages, labels, lengths, candidates, feedback, idf):
    dma = pltpu.SemaphoreType.DMA
    anywhere = pl.BlockSpec(memory_space=pl.ANY)
    scores = pl.pallas_call(
        kernel,
        out_shape=jax.ShapeDtypeStruct((2, NCAND), F32),
        in_specs=[anywhere] * 7,
        out_specs=pl.BlockSpec(memory_space=pltpu.VMEM),
        scratch_shapes=[
            pltpu.SMEM((NY,), jnp.int32),
            pltpu.VMEM((PLANE, QTOK, D), BF16),
            pltpu.VMEM((PTOK, D), BF16),
            pltpu.VMEM((NZ, PTOK, D), BF16),
            pltpu.VMEM((NY, PTOK), jnp.int32),
            pltpu.VMEM((1, NCAND), jnp.int32),
            pltpu.VMEM((FB, NZ * ROW), jnp.int32),
            pltpu.VMEM((NCLUS, NZ * ROW), jnp.int32),
            pltpu.VMEM((PLANE, CPAD, D), F32),
            pltpu.VMEM((EXP, EROWS), BF16),
            pltpu.VMEM((NZ, CPAD, D), F32),
            pltpu.VMEM((NZ, CPAD, D), F32),
            pltpu.VMEM((PLANE, CPAD, D), BF16),
            pltpu.VMEM((NZ, QROWS + EROWS), F32),
            pltpu.VMEM((PLANE, D), F32),
            pltpu.VMEM((PLANE, D), F32),
            dma((7,)),
            dma, dma((ROW,)), dma,
            dma, dma, dma,
            dma, dma((NZ * CHUNKS // 2,)), dma, dma,
            dma, dma,
            dma, dma,
            dma, dma,
            pltpu.SemaphoreType.REGULAR,
            pltpu.SemaphoreType.REGULAR,
        ],
        compiler_params=pltpu.CompilerParams(collective_id=0, has_side_effects=True),
    )(queries, passages, labels, lengths, candidates, feedback.T, idf.T)
    return scores[0:1], scores[1:2]


def solution(mesh):
    return jax.shard_map(
        local,
        mesh=mesh,
        in_specs=(
            P(("rep", "shard"), None, None),
            P(("shard", "rep"), None, None),
            P("shard", None),
            P("shard"),
            P(("rep", "shard"), None),
            P("rep", None),
            P("rep", None),
        ),
        out_specs=(P(("rep", "shard"), None), P(("rep", "shard"), None)),
        check_vma=False,
    )
```

```python
import functools

import jax
import jax.numpy as jnp
from jax import lax
from jax.experimental import pallas as pl
from jax.experimental.pallas import tpu as pltpu
from jax.sharding import PartitionSpec as P

MESH = pl.DeviceIdType.MESH
F32 = jnp.float32
BF16 = jnp.bfloat16
NT = (((1,), (1,)), ((), ()))

NZ, NX, NY, NC = 16, 4, 4, 2
PLANE = NX * NY * NC
ROW = NX * NC
QTOK, PTOK, D = 32, 128, 128
NCLUS, CPAD, FB = 10, 16, 3
TROWS = NCLUS + 1
NCAND = 256
QROWS = PLANE * QTOK
EROWS = PLANE * NCLUS
EXP = NZ * NCLUS
TILE = 256
GROUP = 4
RS_ORDER = (8, 7, 9, 6, 10, 5, 11, 4, 12, 3, 13, 2, 14, 1, 15)
RELAYS = (
    (0, ((2, 2), (-2, 14), (1, 1), (-1, 15))),
    (2, ((2, 4), (1, 3))),
    (14, ((-2, 12), (-1, 13))),
    (4, ((2, 6), (1, 5))),
    (12, ((-2, 10), (-1, 11))),
    (6, ((2, 8), (1, 7))),
    (10, ((-1, 9),)),
)


def ring(n):
    return min(n, 4 - n)


OFFSETS = sorted(
    [(dy, dx, dc) for dy in range(NY) for dx in range(NX) for dc in range(NC)][1:],
    key=lambda o: -(ring(o[0]) + ring(o[1])),
)


def iota(shape, dim):
    return lax.broadcasted_iota(jnp.int32, shape, dim)


def tenth(a):
    return lax.shift_right_logical(a * 6554, 16)


def eleventh(a):
    return lax.shift_right_logical(a * 5958, 16)


def split3(a):
    hi = a.astype(BF16)
    rest = a - hi.astype(F32)
    mid = rest.astype(BF16)
    low = (rest - mid.astype(F32)).astype(BF16)
    return hi, mid, low


def kernel(
    q_hbm, p_hbm, lab_hbm, len_hbm, cand_hbm, fb_hbm, idf_hbm,
    out_ref,
    len_ref, qbuf, praw, pas, lab, cand, fb, idf, tot, mix, part, rs, exb, best, best_exp, back, ret,
    load_sem, tot_send, tot_recv, query_send, row_query_recv, col_query_recv,
    pas_send, relay_recv, odd_recv, end_recv, rs_send, rs_recv, exp_send, exp_recv, ret_send, ret_recv, near_sem, far_sem, plane_sem,
):
    s = lax.axis_index("shard")
    y = lax.axis_index("rep")
    core = lax.rem(s, 2)
    x = lax.rem(lax.div(s, 2), NX)
    z = lax.div(s, ROW)

    def device(dz=0, dy=0, dx=0, dc=0):
        tz = lax.rem(z + (dz + NZ), NZ)
        ty = lax.rem(y + (dy + NY), NY)
        tx = lax.rem(x + (dx + NX), NX)
        tc = lax.rem(core + dc, 2)
        return ((tz * NX + tx) * NC + tc, ty)

    def remote(src, dst, send, recv, to):
        return pltpu.make_async_remote_copy(
            src_ref=src, dst_ref=dst, send_sem=send, recv_sem=recv, device_id=to, device_id_type=MESH
        )

    row_steps = [(2, 0), (2, 1), (1, 0), (3, 0), (1, 1), (3, 1), (0, 1)]
    barrier = pltpu.get_barrier_semaphore()
    near = [device(dz=dz) for dz in (2, -2)] + [device(dy=2)]
    near += [device(dx=dx, dc=dc) for dx, dc in row_steps]
    near += [device(dy=dy) for dy in (1, 3)]
    near += [device(dz=dz) for dz in (1, -1)]
    for to in near:
        pl.semaphore_signal(barrier, inc=1, device_id=to, device_id_type=MESH)

    loads = [
        pltpu.make_async_copy(src, dst, load_sem.at[i])
        for i, (src, dst) in enumerate(
            (
                (p_hbm.at[0], praw),
                (lab_hbm, lab),
                (q_hbm.at[0], qbuf.at[0]),
                (idf_hbm, idf),
                (fb_hbm, fb),
                (cand_hbm, cand),
                (len_hbm, len_ref),
            )
        )
    ]
    for copy in loads:
        copy.start()

    loads[6].wait()
    length = len_ref[y]
    loads[1].wait()
    loads[0].wait()
    passage = praw[...]
    labels = lab[pl.ds(y, 1), :]
    picked = (iota((CPAD, PTOK), 0) == labels) & (iota((CPAD, PTOK), 1) < length)
    totals = jnp.dot(
        jnp.where(picked, 1.0, 0.0).astype(BF16), passage, preferred_element_type=F32
    )
    wide = passage.astype(F32)
    masked = jnp.where(iota((PTOK, D), 0) < length, wide, wide[0:1, :])
    pas[0] = masked.astype(BF16)
    loads[2].wait()
    loads[3].wait()
    mine = jnp.where(
        (iota((CPAD, NZ * ROW), 1) == s) & (iota((CPAD, NZ * ROW), 0) == NCLUS), 1.0, 0.0
    ).astype(BF16)
    spread = jnp.where(
        iota((NCLUS, D), 0) == iota((NCLUS, D), 1), 1.0, 0.0
    ).astype(BF16)
    table = lax.dot_general(
        idf[...].astype(F32).astype(BF16), spread, (((0,), (0,)), ((), ())),
        preferred_element_type=F32,
    ).astype(BF16)
    tot[0:TROWS] = (totals + jnp.dot(mine, table, preferred_element_type=F32))[:TROWS]
    back[...] = jnp.zeros_like(back)

    pl.semaphore_wait(barrier, len(near))

    def arrive(ref, sem):
        remote(ref, ref, sem, sem, device(dc=1)).wait_recv()

    def leave(ref, sem):
        remote(ref, ref, sem, sem, device(dc=1)).wait_send()

    for dz in (2, -2):
        pl.semaphore_signal(near_sem, inc=1, device_id=device(dz=dz), device_id_type=MESH)

    def place(slot):
        return slot // 2 + (slot % 2) * (NZ // 2)

    def pass_recv(slot):
        if slot % 2:
            return odd_recv
        return end_recv if slot == NZ // 2 else relay_recv.at[(slot % (NZ // 2)) // 2 - 1 + 3 * (slot // (NZ // 2))]

    def relay(entry):
        source, hops = entry
        if source:
            arrive(pas.at[place(source)], pass_recv(source))
        for dz, slot in hops:
            remote(
                pas.at[place(source)], pas.at[place(slot)],
                pas_send, pass_recv(slot), device(dz=dz),
            ).start()

    for dy in (2, 1, 3):
        pl.semaphore_signal(plane_sem, inc=1, device_id=device(dy=dy), device_id_type=MESH)

    def rows_of(slot, count=1):
        return pl.ds(slot * TROWS, count * TROWS)

    def tot_send_to(dy, dx, dc):
        slot = dy * ROW + dx * NC + dc
        remote(
            tot.at[rows_of(0)], tot.at[rows_of(slot)], tot_send, tot_recv,
            device(dy=dy, dx=dx, dc=dc),
        ).start()

    for dx, dc in row_steps:
        tot_send_to(0, dx, dc)
    for dy in (2, 1, 3):
        tot_send_to(dy, 0, 0)
    relay(RELAYS[0])
    pl.semaphore_wait(plane_sem, 3)
    for dy, dx, dc in OFFSETS:
        if dy and (dx or dc):
            tot_send_to(dy, dx, dc)
    loads[4].wait()
    loads[5].wait()
    turn = lax.rem(iota((NZ, NZ * ROW), 0) + z, NZ) * ROW + (x * NC + core)
    pick = jnp.where(iota((NZ, NZ * ROW), 1) == turn, 1.0, 0.0).astype(F32)
    ids = lax.dot_general(
        pick, fb[...].astype(F32), NT,
        precision=lax.Precision.HIGHEST, preferred_element_type=F32,
    )
    slots = iota((NZ, PLANE), 1)
    slot_y = lax.rem(y + NY - lax.div(slots, ROW), NY)
    slot_x = lax.rem(x + NX - lax.rem(lax.div(slots, NC), NX), NX)
    slot_c = lax.rem(core + lax.rem(slots, NC), 2)
    slot_id = (z * PLANE + slot_x * (NC * NY) + slot_c * NY + slot_y).astype(F32)
    counts = jnp.zeros((NZ, PLANE), F32)
    for k in range(FB):
        counts += jnp.where(jnp.abs(slot_id - ids[:, k : k + 1]) < 0.5, 1.0, 0.0)
    up = jnp.where(tenth(iota((EXP, NZ), 0)) == iota((EXP, NZ), 1), 1.0, 0.0).astype(BF16)
    wide_shape = (PLANE, PLANE * TROWS)
    over = jnp.where(eleventh(iota(wide_shape, 1)) == iota(wide_shape, 0), 1.0, 0.0).astype(BF16)
    tall = jnp.dot(up, counts.astype(BF16), preferred_element_type=F32).astype(BF16)
    counts = jnp.dot(tall, over, preferred_element_type=F32)
    to, at = iota((EXP, PLANE * TROWS), 0), iota((EXP, PLANE * TROWS), 1)
    same = to - NCLUS * tenth(to) == at - TROWS * eleventh(at)
    mix[...] = jnp.where(same, counts, 0.0).astype(BF16)

    for dx, dc in row_steps:
        slot = dx * NC + dc
        remote(
            qbuf.at[0], qbuf.at[slot], query_send, row_query_recv, device(dx=dx, dc=dc)
        ).start()
    pl.semaphore_wait(near_sem, 2)
    for dz in (4, -4):
        pl.semaphore_signal(far_sem, inc=1, device_id=device(dz=dz), device_id_type=MESH)
    relay(RELAYS[1])
    relay(RELAYS[2])
    arrive(tot.at[rows_of(1, PLANE - 1)], tot_recv)

    counts = mix[...]
    summed = None
    for piece in split3(tot[...]):
        term = jnp.dot(counts, piece, preferred_element_type=F32)
        summed = term if summed is None else summed + term
    part[...] = summed
    pl.semaphore_wait(far_sem, 2)
    for dz in RS_ORDER:
        remote(
            part.at[pl.ds(dz * NCLUS, NCLUS)], rs.at[dz, pl.ds(0, NCLUS)],
            rs_send, rs_recv, device(dz=dz),
        ).start()
    arrive(qbuf.at[pl.ds(1, ROW - 1)], row_query_recv)
    for dy in (2, 1, 3):
        remote(
            qbuf.at[pl.ds(0, ROW)], qbuf.at[pl.ds(dy * ROW, ROW)],
            query_send, col_query_recv, device(dy=dy),
        ).start()

    lanes = iota((D, EROWS), 1)
    spread = jnp.where(lanes - NCLUS * tenth(lanes) == iota((D, EROWS), 0), 1.0, 0.0).astype(BF16)
    idf_rows = tot[pl.ds(NCLUS, PLANE, stride=TROWS), :].astype(BF16)
    idf_rows = jnp.dot(idf_rows, spread, preferred_element_type=F32)
    owner = tenth(iota((PLANE, EROWS), 1))
    exp_weight = jnp.where(owner == iota((PLANE, EROWS), 0), idf_rows, 0.0).astype(BF16)
    query_weight = jnp.where(
        lax.div(iota((PLANE, QROWS), 1), QTOK) == iota((PLANE, QROWS), 0), 1.0, 0.0
    ).astype(BF16)

    for entry in RELAYS[3:]:
        relay(entry)

    arrive(rs.at[pl.ds(1, NZ - 1), pl.ds(0, NCLUS)], rs_recv)
    rows = part[0:NCLUS]
    for dz in range(1, NZ):
        rows += rs[dz, 0:NCLUS]
    factor = lax.rsqrt(jnp.mean(rows * rows, axis=1, keepdims=True) + 1e-06)
    exb[0:NCLUS] = (rows * factor).astype(BF16)
    for dy, dx, dc in OFFSETS:
        slot = dy * ROW + dx * NC + dc
        remote(
            exb.at[pl.ds(0, NCLUS)], exb.at[pl.ds(slot * NCLUS, NCLUS)], exp_send, exp_recv,
            device(dy=dy, dx=dx, dc=dc),
        ).start()

    arrive(qbuf.at[pl.ds(ROW, PLANE - ROW)], col_query_recv)
    arrive(pas.at[pl.ds(NZ // 2, NZ // 2)], odd_recv)
    arrive(pas.at[NZ // 4], end_recv)

    def score(vectors, out, at):
        for n in range(0, NZ, GROUP):
            tokens = pas[n : n + GROUP].reshape(GROUP * PTOK, D)
            scores = lax.dot_general(tokens, vectors, NT, preferred_element_type=F32)
            for m in range(GROUP):
                top = jnp.max(scores[m * PTOK : (m + 1) * PTOK], axis=0, keepdims=True)
                out[n + m : n + m + 1, at : at + vectors.shape[0]] = top

    for tile in range(QROWS // TILE):
        vectors = qbuf[tile * ROW : (tile + 1) * ROW].reshape(TILE, D)
        score(vectors, best, tile * TILE)

    def reduce(weight, values):
        hi, mid, low = split3(values)
        total = lax.dot_general(weight, hi, NT, preferred_element_type=F32)
        total += lax.dot_general(weight, mid, NT, preferred_element_type=F32)
        return total + lax.dot_general(weight, low, NT, preferred_element_type=F32)

    plain = reduce(query_weight, best[...]) * (1.0 / QTOK)
    back[:, 0:NZ] = plain

    ids = cand[...]
    cand_y = lax.rem(ids, NY)
    cand_c = lax.rem(lax.div(ids, NY), NC)
    cand_x = lax.rem(lax.div(ids, NY * NC), NX)
    cand_z = lax.div(ids, PLANE)
    cand_slot = (
        lax.rem(cand_y + NY - y, NY) * ROW
        + lax.rem(cand_x + NX - x, NX) * NC
        + lax.rem(cand_c + core, 2)
    )
    cand_n = lax.rem(z + NZ - cand_z, NZ)
    cand_n = lax.div(cand_n, 2) + lax.rem(cand_n, 2) * (NZ // 2)
    slot_hot = jnp.where(iota((PLANE, NCAND), 0) == cand_slot, 1.0, 0.0).astype(BF16)
    n_hot = iota((NZ, NCAND), 0) == cand_n

    arrive(exb.at[pl.ds(NCLUS, EROWS - NCLUS)], exp_recv)
    for at in range(0, EROWS, TILE):
        score(exb[at : min(at + TILE, EROWS)], best_exp, at)
    added = reduce(exp_weight, best_exp[...]) * (1.0 / (8.0 * NCLUS))
    back[:, NZ : 2 * NZ] = plain + added

    for dy, dx, dc in OFFSETS:
        slot = dy * ROW + dx * NC + dc
        remote(
            back.at[pl.ds(slot, 1)], ret.at[pl.ds(slot, 1)], ret_send, ret_recv,
            device(dy=-dy, dx=-dx, dc=dc),
        ).start()
    ret[0:1, :] = back[0:1, :]
    others = pl.ds(1, PLANE - 1)
    leave(tot.at[rows_of(1, PLANE - 1)], tot_send)
    leave(qbuf.at[others], query_send)
    leave(pas.at[pl.ds(1, NZ - 1)], pas_send)
    leave(rs.at[pl.ds(1, NZ - 1), pl.ds(0, NCLUS)], rs_send)
    leave(exb.at[pl.ds(NCLUS, EROWS - NCLUS)], exp_send)
    arrive(ret.at[others], ret_recv)
    flat = ret[...].T[: 2 * NZ, :]
    chosen = None
    for piece in split3(flat):
        term = jnp.dot(piece, slot_hot, preferred_element_type=F32)
        chosen = term if chosen is None else chosen + term
    out_ref[0:1, :] = jnp.sum(jnp.where(n_hot, chosen[:NZ], 0.0), axis=0, keepdims=True)
    out_ref[1:2, :] = jnp.sum(jnp.where(n_hot, chosen[NZ:], 0.0), axis=0, keepdims=True)
    leave(ret.at[others], ret_send)


def local(queries, passages, labels, lengths, candidates, feedback, idf):
    dma = pltpu.SemaphoreType.DMA
    anywhere = pl.BlockSpec(memory_space=pl.ANY)
    scores = pl.pallas_call(
        kernel,
        out_shape=pltpu.VMEM((2, NCAND), F32),
        in_specs=[anywhere] * 7,
        out_specs=pl.BlockSpec(memory_space=pltpu.VMEM),
        scratch_shapes=[
            pltpu.SMEM((NY,), jnp.int32),
            pltpu.VMEM((PLANE, QTOK, D), BF16),
            pltpu.VMEM((PTOK, D), BF16),
            pltpu.VMEM((NZ, PTOK, D), BF16),
            pltpu.VMEM((NY, PTOK), jnp.int32),
            pltpu.VMEM((1, NCAND), jnp.int32),
            pltpu.VMEM((FB, NZ * ROW), jnp.int32),
            pltpu.VMEM((NCLUS, NZ * ROW), jnp.int32),
            pltpu.VMEM((PLANE * TROWS, D), F32),
            pltpu.VMEM((EXP, PLANE * TROWS), BF16),
            pltpu.VMEM((EXP, D), F32),
            pltpu.VMEM((NZ, CPAD, D), F32),
            pltpu.VMEM((EROWS, D), BF16),
            pltpu.VMEM((NZ, QROWS), F32),
            pltpu.VMEM((NZ, EROWS), F32),
            pltpu.VMEM((PLANE, D), F32),
            pltpu.VMEM((PLANE, D), F32),
            dma((7,)),
            dma, dma,
            dma, dma, dma,
            dma, dma((6,)), dma, dma,
            dma, dma,
            dma, dma,
            dma, dma,
            pltpu.SemaphoreType.REGULAR,
            pltpu.SemaphoreType.REGULAR,
            pltpu.SemaphoreType.REGULAR,
        ],
        compiler_params=pltpu.CompilerParams(collective_id=0, has_side_effects=True),
    )(queries, passages, labels, lengths, candidates, feedback.T, idf.T)
    return scores[0:1], scores[1:2]


def solution(mesh):
    return jax.shard_map(
        local,
        mesh=mesh,
        in_specs=(
            P(("rep", "shard"), None, None),
            P(("shard", "rep"), None, None),
            P("shard", None),
            P("shard"),
            P(("rep", "shard"), None),
            P("rep", None),
            P("rep", None),
        ),
        out_specs=(P(("rep", "shard"), None), P(("rep", "shard"), None)),
        check_vma=False,
    )
```

```python
import functools

import jax
import jax.numpy as jnp
from jax import lax
from jax.experimental import pallas as pl
from jax.experimental.pallas import tpu as pltpu
from jax.sharding import PartitionSpec as P

MESH = pl.DeviceIdType.MESH
F32 = jnp.float32
BF16 = jnp.bfloat16
NT = (((1,), (1,)), ((), ()))

NZ, NX, NY, NC = 16, 4, 4, 2
PLANE = NX * NY * NC
ROW = NX * NC
QTOK, PTOK, D = 32, 128, 128
NCLUS, CPAD, FB = 10, 16, 3
TROWS = NCLUS + 1
NCAND = 256
QROWS = PLANE * QTOK
EROWS = PLANE * NCLUS
EXP = NZ * NCLUS
TILE = 256
GROUP = 4
LATE_RELAYS = 3
RELAYS = (
    (0, ((2, 2), (-2, 14), (1, 1), (-1, 15))),
    (2, ((2, 4), (1, 3))),
    (14, ((-2, 12), (-1, 13))),
    (4, ((2, 6), (1, 5))),
    (12, ((-2, 10), (-1, 11))),
    (6, ((1, 7),)),
    (10, ((-2, 8), (-1, 9))),
)

RELAYED = [source for source, _ in RELAYS]
PLACES = RELAYED + [1, 15, 3, 13, 5, 11, 7, 9, 8]
HELD, LAST = len(RELAYED), NZ - 3


def ring(n):
    return min(n, 4 - n)


OFFSETS = sorted(
    [(dy, dx, dc) for dy in range(NY) for dx in range(NX) for dc in range(NC)][1:],
    key=lambda o: -(ring(o[0]) + ring(o[1])),
)


def iota(shape, dim):
    return lax.broadcasted_iota(jnp.int32, shape, dim)


def tenth(a):
    return lax.shift_right_logical(a * 6554, 16)


def eleventh(a):
    return lax.shift_right_logical(a * 5958, 16)


def split3(a):
    hi = a.astype(BF16)
    rest = a - hi.astype(F32)
    mid = rest.astype(BF16)
    low = (rest - mid.astype(F32)).astype(BF16)
    return hi, mid, low


def kernel(
    q_hbm, p_hbm, lab_hbm, len_hbm, cand_hbm, fb_hbm, idf_hbm,
    out_ref,
    len_ref, qbuf, praw, pas, lab, cand, fb, idf, tot, mix, part, rs, exb, best, best_exp, back, ret,
    load_sem, tot_send, tot_recv, query_send, row_query_recv, col_query_recv,
    pas_send, relay_recv, rest_recv, rs_send, rs_recv, exp_send, exp_recv, ret_send, ret_recv, near_sem, far_sem, plane_sem,
):
    s = lax.axis_index("shard")
    y = lax.axis_index("rep")
    core = lax.rem(s, 2)
    x = lax.rem(lax.div(s, 2), NX)
    z = lax.div(s, ROW)

    def device(dz=0, dy=0, dx=0, dc=0):
        tz = lax.rem(z + (dz + NZ), NZ)
        ty = lax.rem(y + (dy + NY), NY)
        tx = lax.rem(x + (dx + NX), NX)
        tc = lax.rem(core + dc, 2)
        return ((tz * NX + tx) * NC + tc, ty)

    def remote(src, dst, send, recv, to):
        return pltpu.make_async_remote_copy(
            src_ref=src, dst_ref=dst, send_sem=send, recv_sem=recv, device_id=to, device_id_type=MESH
        )

    row_steps = [(2, 0), (2, 1), (1, 0), (3, 0), (1, 1), (3, 1), (0, 1)]
    barrier = pltpu.get_barrier_semaphore()
    near = [device(dz=dz) for dz in (2, -2)] + [device(dy=2)]
    near += [device(dx=dx, dc=dc) for dx, dc in row_steps]
    near += [device(dy=dy) for dy in (1, 3)]
    near += [device(dz=dz) for dz in (1, -1)]
    for to in near:
        pl.semaphore_signal(barrier, inc=1, device_id=to, device_id_type=MESH)

    loads = [
        pltpu.make_async_copy(src, dst, load_sem.at[i])
        for i, (src, dst) in enumerate(
            (
                (p_hbm.at[0], praw),
                (lab_hbm, lab),
                (q_hbm.at[0], qbuf.at[0]),
                (idf_hbm, idf),
                (fb_hbm, fb),
                (cand_hbm, cand),
                (len_hbm, len_ref),
            )
        )
    ]
    for copy in loads:
        copy.start()

    loads[6].wait()
    length = len_ref[y]
    loads[1].wait()
    loads[0].wait()
    passage = praw[...]
    labels = lab[pl.ds(y, 1), :]
    picked = (iota((CPAD, PTOK), 0) == labels) & (iota((CPAD, PTOK), 1) < length)
    totals = jnp.dot(
        jnp.where(picked, 1.0, 0.0).astype(BF16), passage, preferred_element_type=F32
    )
    wide = passage.astype(F32)
    masked = jnp.where(iota((PTOK, D), 0) < length, wide, wide[0:1, :])
    pas[0] = masked.astype(BF16)
    loads[2].wait()
    loads[3].wait()
    mine = jnp.where(
        (iota((CPAD, NZ * ROW), 1) == s) & (iota((CPAD, NZ * ROW), 0) == NCLUS), 1.0, 0.0
    ).astype(BF16)
    spread = jnp.where(
        iota((NCLUS, D), 0) == iota((NCLUS, D), 1), 1.0, 0.0
    ).astype(BF16)
    table = lax.dot_general(
        idf[...].astype(F32).astype(BF16), spread, (((0,), (0,)), ((), ())),
        preferred_element_type=F32,
    ).astype(BF16)
    tot[0:TROWS] = (totals + jnp.dot(mine, table, preferred_element_type=F32))[:TROWS]
    back[...] = jnp.zeros_like(back)

    pl.semaphore_wait(barrier, len(near))

    def arrive(ref, sem):
        remote(ref, ref, sem, sem, device(dc=1)).wait_recv()

    def leave(ref, sem):
        remote(ref, ref, sem, sem, device(dc=1)).wait_send()

    for dz in (2, -2):
        pl.semaphore_signal(near_sem, inc=1, device_id=device(dz=dz), device_id_type=MESH)

    def place(slot):
        return PLACES.index(slot)

    def pass_recv(slot):
        at = place(slot)
        return relay_recv.at[at] if at < HELD else rest_recv.at[at // LAST]

    def relay(entry):
        source, hops = entry
        if source:
            arrive(pas.at[place(source)], pass_recv(source))
        for dz, slot in hops:
            remote(
                pas.at[place(source)], pas.at[place(slot)],
                pas_send, pass_recv(slot), device(dz=dz),
            ).start()

    for dy in (2, 1, 3):
        pl.semaphore_signal(plane_sem, inc=1, device_id=device(dy=dy), device_id_type=MESH)

    def rows_of(slot, count=1):
        return pl.ds(slot * TROWS, count * TROWS)

    def tot_send_to(dy, dx, dc):
        slot = dy * ROW + dx * NC + dc
        remote(
            tot.at[rows_of(0)], tot.at[rows_of(slot)], tot_send, tot_recv,
            device(dy=dy, dx=dx, dc=dc),
        ).start()

    for dx, dc in row_steps:
        tot_send_to(0, dx, dc)
    for dy in (2, 1, 3):
        tot_send_to(dy, 0, 0)
    relay(RELAYS[0])
    pl.semaphore_wait(plane_sem, 3)
    for dy, dx, dc in OFFSETS:
        if dy and (dx or dc):
            tot_send_to(dy, dx, dc)
    loads[4].wait()
    loads[5].wait()
    turn = lax.rem(iota((NZ, NZ * ROW), 0) + z, NZ) * ROW + (x * NC + core)
    pick = jnp.where(iota((NZ, NZ * ROW), 1) == turn, 1.0, 0.0).astype(F32)
    ids = lax.dot_general(
        pick, fb[...].astype(F32), NT,
        precision=lax.Precision.HIGHEST, preferred_element_type=F32,
    )
    slots = iota((NZ, PLANE), 1)
    slot_y = lax.rem(y + NY - lax.div(slots, ROW), NY)
    slot_x = lax.rem(x + NX - lax.rem(lax.div(slots, NC), NX), NX)
    slot_c = lax.rem(core + lax.rem(slots, NC), 2)
    slot_id = (z * PLANE + slot_x * (NC * NY) + slot_c * NY + slot_y).astype(F32)
    counts = jnp.zeros((NZ, PLANE), F32)
    for k in range(FB):
        counts += jnp.where(jnp.abs(slot_id - ids[:, k : k + 1]) < 0.5, 1.0, 0.0)
    up = jnp.where(tenth(iota((EXP, NZ), 0)) == iota((EXP, NZ), 1), 1.0, 0.0).astype(BF16)
    wide_shape = (PLANE, PLANE * TROWS)
    over = jnp.where(eleventh(iota(wide_shape, 1)) == iota(wide_shape, 0), 1.0, 0.0).astype(BF16)
    tall = jnp.dot(up, counts.astype(BF16), preferred_element_type=F32).astype(BF16)
    counts = jnp.dot(tall, over, preferred_element_type=F32)
    to, at = iota((EXP, PLANE * TROWS), 0), iota((EXP, PLANE * TROWS), 1)
    same = to - NCLUS * tenth(to) == at - TROWS * eleventh(at)
    mix[...] = jnp.where(same, counts, 0.0).astype(BF16)

    for dx, dc in row_steps:
        slot = dx * NC + dc
        remote(
            qbuf.at[0], qbuf.at[slot], query_send, row_query_recv, device(dx=dx, dc=dc)
        ).start()
    pl.semaphore_wait(near_sem, 2)
    for dz in (4, -4):
        pl.semaphore_signal(far_sem, inc=1, device_id=device(dz=dz), device_id_type=MESH)
    for entry in RELAYS[1:LATE_RELAYS]:
        relay(entry)
    arrive(tot.at[rows_of(1, PLANE - 1)], tot_recv)

    counts = mix[...]
    summed = None
    for piece in split3(tot[...]):
        term = jnp.dot(counts, piece, preferred_element_type=F32)
        summed = term if summed is None else summed + term
    for dz in range(NZ):
        part[dz, 0:NCLUS] = summed[dz * NCLUS : (dz + 1) * NCLUS]
    pl.semaphore_wait(far_sem, 2)
    for k in range(NZ - 1):
        target = k + lax.div(k + NZ - z, NZ)
        dz = lax.rem(target + NZ - z, NZ)
        remote(
            part.at[dz, pl.ds(0, NCLUS)], rs.at[dz, pl.ds(0, NCLUS)],
            rs_send, rs_recv, device(dz=dz),
        ).start()
    arrive(qbuf.at[pl.ds(1, ROW - 1)], row_query_recv)
    for dy in (2, 1, 3):
        remote(
            qbuf.at[pl.ds(0, ROW)], qbuf.at[pl.ds(dy * ROW, ROW)],
            query_send, col_query_recv, device(dy=dy),
        ).start()

    lanes = iota((D, EROWS), 1)
    spread = jnp.where(lanes - NCLUS * tenth(lanes) == iota((D, EROWS), 0), 1.0, 0.0).astype(BF16)
    idf_rows = tot[pl.ds(NCLUS, PLANE, stride=TROWS), :].astype(BF16)
    idf_rows = jnp.dot(idf_rows, spread, preferred_element_type=F32)
    owner = tenth(iota((PLANE, EROWS), 1))
    exp_weight = jnp.where(owner == iota((PLANE, EROWS), 0), idf_rows, 0.0).astype(BF16)
    query_weight = jnp.where(
        lax.div(iota((PLANE, QROWS), 1), QTOK) == iota((PLANE, QROWS), 0), 1.0, 0.0
    ).astype(BF16)

    for entry in RELAYS[LATE_RELAYS:]:
        relay(entry)

    arrive(rs.at[pl.ds(1, NZ - 1), pl.ds(0, NCLUS)], rs_recv)
    rows = part[0, 0:NCLUS]
    for dz in range(1, NZ):
        rows += rs[dz, 0:NCLUS]
    factor = lax.rsqrt(jnp.mean(rows * rows, axis=1, keepdims=True) + 1e-06)
    exb[0:NCLUS] = (rows * factor).astype(BF16)
    for dy, dx, dc in OFFSETS:
        slot = dy * ROW + dx * NC + dc
        remote(
            exb.at[pl.ds(0, NCLUS)], exb.at[pl.ds(slot * NCLUS, NCLUS)], exp_send, exp_recv,
            device(dy=dy, dx=dx, dc=dc),
        ).start()

    arrive(qbuf.at[pl.ds(ROW, PLANE - ROW)], col_query_recv)
    def score(vectors, out, at, first, last):
        for n in range(first, last, GROUP):
            stop = min(n + GROUP, last)
            tokens = pas[n:stop].reshape((stop - n) * PTOK, D)
            scores = lax.dot_general(tokens, vectors, NT, preferred_element_type=F32)
            for m in range(n, stop):
                top = scores[(m - n) * PTOK : (m - n + 1) * PTOK]
                out[m : m + 1, at : at + vectors.shape[0]] = jnp.max(top, axis=0, keepdims=True)

    def plain_score(first, last):
        for tile in range(QROWS // TILE):
            vectors = qbuf[tile * ROW : (tile + 1) * ROW].reshape(TILE, D)
            score(vectors, best, tile * TILE, first, last)

    plain_score(0, HELD)
    arrive(pas.at[pl.ds(HELD, LAST - HELD)], rest_recv.at[0])
    plain_score(HELD, LAST)
    arrive(pas.at[pl.ds(LAST, NZ - LAST)], rest_recv.at[1])
    plain_score(LAST, NZ)

    def reduce(weight, values):
        hi, mid, low = split3(values)
        total = lax.dot_general(weight, hi, NT, preferred_element_type=F32)
        total += lax.dot_general(weight, mid, NT, preferred_element_type=F32)
        return total + lax.dot_general(weight, low, NT, preferred_element_type=F32)

    plain = reduce(query_weight, best[...]) * (1.0 / QTOK)
    back[:, 0:NZ] = plain

    ids = cand[...]
    cand_y = lax.rem(ids, NY)
    cand_c = lax.rem(lax.div(ids, NY), NC)
    cand_x = lax.rem(lax.div(ids, NY * NC), NX)
    cand_z = lax.div(ids, PLANE)
    cand_slot = (
        lax.rem(cand_y + NY - y, NY) * ROW
        + lax.rem(cand_x + NX - x, NX) * NC
        + lax.rem(cand_c + core, 2)
    )
    cand_n = lax.rem(z + NZ - cand_z, NZ)
    slot_hot = jnp.where(iota((PLANE, NCAND), 0) == cand_slot, 1.0, 0.0).astype(BF16)
    held = iota((NZ, NCAND), 0)
    slot_at = jnp.zeros((NZ, NCAND), jnp.int32)
    for at, slot in enumerate(PLACES):
        slot_at = jnp.where(held == at, slot, slot_at)
    n_hot = slot_at == cand_n

    arrive(exb.at[pl.ds(NCLUS, EROWS - NCLUS)], exp_recv)
    for at in range(0, EROWS, TILE):
        score(exb[at : min(at + TILE, EROWS)], best_exp, at, 0, NZ)
    added = reduce(exp_weight, best_exp[...]) * (1.0 / (8.0 * NCLUS))
    back[:, NZ : 2 * NZ] = plain + added

    for dy, dx, dc in OFFSETS:
        slot = dy * ROW + dx * NC + dc
        remote(
            back.at[pl.ds(slot, 1)], ret.at[pl.ds(slot, 1)], ret_send, ret_recv,
            device(dy=-dy, dx=-dx, dc=dc),
        ).start()
    ret[0:1, :] = back[0:1, :]
    others = pl.ds(1, PLANE - 1)
    leave(tot.at[rows_of(1, PLANE - 1)], tot_send)
    leave(qbuf.at[others], query_send)
    leave(pas.at[pl.ds(1, NZ - 1)], pas_send)
    leave(rs.at[pl.ds(1, NZ - 1), pl.ds(0, NCLUS)], rs_send)
    leave(exb.at[pl.ds(NCLUS, EROWS - NCLUS)], exp_send)
    arrive(ret.at[others], ret_recv)
    flat = ret[...].T[: 2 * NZ, :]
    chosen = None
    for piece in split3(flat):
        term = jnp.dot(piece, slot_hot, preferred_element_type=F32)
        chosen = term if chosen is None else chosen + term
    out_ref[0:1, :] = jnp.sum(jnp.where(n_hot, chosen[:NZ], 0.0), axis=0, keepdims=True)
    out_ref[1:2, :] = jnp.sum(jnp.where(n_hot, chosen[NZ:], 0.0), axis=0, keepdims=True)
    leave(ret.at[others], ret_send)


def local(queries, passages, labels, lengths, candidates, feedback, idf):
    dma = pltpu.SemaphoreType.DMA
    anywhere = pl.BlockSpec(memory_space=pl.ANY)
    scores = pl.pallas_call(
        kernel,
        out_shape=pltpu.VMEM((2, NCAND), F32),
        in_specs=[anywhere] * 7,
        out_specs=pl.BlockSpec(memory_space=pltpu.VMEM),
        scratch_shapes=[
            pltpu.SMEM((NY,), jnp.int32),
            pltpu.VMEM((PLANE, QTOK, D), BF16),
            pltpu.VMEM((PTOK, D), BF16),
            pltpu.VMEM((NZ, PTOK, D), BF16),
            pltpu.VMEM((NY, PTOK), jnp.int32),
            pltpu.VMEM((1, NCAND), jnp.int32),
            pltpu.VMEM((FB, NZ * ROW), jnp.int32),
            pltpu.VMEM((NCLUS, NZ * ROW), jnp.int32),
            pltpu.VMEM((PLANE * TROWS, D), F32),
            pltpu.VMEM((EXP, PLANE * TROWS), BF16),
            pltpu.VMEM((NZ, CPAD, D), F32),
            pltpu.VMEM((NZ, CPAD, D), F32),
            pltpu.VMEM((EROWS, D), BF16),
            pltpu.VMEM((NZ, QROWS), F32),
            pltpu.VMEM((NZ, EROWS), F32),
            pltpu.VMEM((PLANE, D), F32),
            pltpu.VMEM((PLANE, D), F32),
            dma((7,)),
            dma, dma,
            dma, dma, dma,
            dma, dma((HELD,)), dma((2,)),
            dma, dma,
            dma, dma,
            dma, dma,
            pltpu.SemaphoreType.REGULAR,
            pltpu.SemaphoreType.REGULAR,
            pltpu.SemaphoreType.REGULAR,
        ],
        compiler_params=pltpu.CompilerParams(collective_id=0, has_side_effects=True),
    )(queries, passages, labels, lengths, candidates, feedback.T, idf.T)
    return scores[0:1], scores[1:2]


def solution(mesh):
    return jax.shard_map(
        local,
        mesh=mesh,
        in_specs=(
            P(("rep", "shard"), None, None),
            P(("shard", "rep"), None, None),
            P("shard", None),
            P("shard"),
            P(("rep", "shard"), None),
            P("rep", None),
            P("rep", None),
        ),
        out_specs=(P(("rep", "shard"), None), P(("rep", "shard"), None)),
        check_vma=False,
    )
```

```python
import functools

import jax
import jax.numpy as jnp
from jax import lax
from jax.experimental import pallas as pl
from jax.experimental.pallas import tpu as pltpu
from jax.sharding import PartitionSpec as P

MESH = pl.DeviceIdType.MESH
F32 = jnp.float32
BF16 = jnp.bfloat16
NT = (((1,), (1,)), ((), ()))

NZ, NX, NY, NC = 16, 4, 4, 2
PLANE = NX * NY * NC
ROW = NX * NC
QTOK, PTOK, D = 32, 128, 128
NCLUS, CPAD, FB = 10, 16, 3
TROWS = NCLUS + 1
NCAND = 256
QROWS = PLANE * QTOK
EROWS = PLANE * NCLUS
EXP = NZ * NCLUS
TILE = 256
GROUP = 8
LATE_RELAYS = 3
FIRST = 8
RELAYS = (
    (0, ((2, 2), (-2, 14), (1, 1), (-1, 15))),
    (2, ((2, 4), (1, 3))),
    (14, ((-2, 12), (-1, 13))),
    (4, ((2, 6), (1, 5))),
    (12, ((-2, 10), (-1, 11))),
    (6, ((1, 7),)),
    (10, ((-2, 8), (-1, 9))),
)

RELAYED = [source for source, _ in RELAYS]
PLACES = RELAYED + [1, 15, 3, 13, 5, 11, 7, 9, 8]
HELD, LAST = len(RELAYED), NZ - 3


def ring(n):
    return min(n, 4 - n)


OFFSETS = sorted(
    [(dy, dx, dc) for dy in range(NY) for dx in range(NX) for dc in range(NC)][1:],
    key=lambda o: -(ring(o[0]) + ring(o[1])),
)


def iota(shape, dim):
    return lax.broadcasted_iota(jnp.int32, shape, dim)


def tenth(a):
    return lax.shift_right_logical(a * 6554, 16)


def eleventh(a):
    return lax.shift_right_logical(a * 5958, 16)


def split3(a):
    hi = a.astype(BF16)
    rest = a - hi.astype(F32)
    mid = rest.astype(BF16)
    low = (rest - mid.astype(F32)).astype(BF16)
    return hi, mid, low


def kernel(
    q_hbm, p_hbm, lab_hbm, len_hbm, cand_hbm, fb_hbm, idf_hbm,
    out_ref,
    len_ref, qbuf, praw, pas, lab, cand, fb, idf, tot, mix, part, rs, exb, best, best_exp, back, ret,
    load_sem, tot_send, tot_recv, query_send, row_query_recv, col_query_recv,
    pas_send, relay_recv, rest_recv, rs_send, rs_recv, exp_send, exp_recv, ret_send, ret_recv, near_sem, far_sem, plane_sem,
):
    s = lax.axis_index("shard")
    y = lax.axis_index("rep")
    core = lax.rem(s, 2)
    x = lax.rem(lax.div(s, 2), NX)
    z = lax.div(s, ROW)

    def device(dz=0, dy=0, dx=0, dc=0):
        tz = lax.rem(z + (dz + NZ), NZ)
        ty = lax.rem(y + (dy + NY), NY)
        tx = lax.rem(x + (dx + NX), NX)
        tc = lax.rem(core + dc, 2)
        return ((tz * NX + tx) * NC + tc, ty)

    def remote(src, dst, send, recv, to):
        return pltpu.make_async_remote_copy(
            src_ref=src, dst_ref=dst, send_sem=send, recv_sem=recv, device_id=to, device_id_type=MESH
        )

    row_steps = [(2, 0), (2, 1), (1, 0), (3, 0), (1, 1), (3, 1), (0, 1)]
    barrier = pltpu.get_barrier_semaphore()
    near = [device(dz=dz) for dz in (2, -2)] + [device(dy=2)]
    near += [device(dx=dx, dc=dc) for dx, dc in row_steps]
    near += [device(dy=dy) for dy in (1, 3)]
    near += [device(dz=dz) for dz in (1, -1)]
    for to in near:
        pl.semaphore_signal(barrier, inc=1, device_id=to, device_id_type=MESH)

    loads = [
        pltpu.make_async_copy(src, dst, load_sem.at[i])
        for i, (src, dst) in enumerate(
            (
                (p_hbm.at[0], praw),
                (lab_hbm, lab),
                (q_hbm.at[0], qbuf.at[0]),
                (idf_hbm, idf),
                (fb_hbm, fb),
                (cand_hbm, cand),
                (len_hbm, len_ref),
            )
        )
    ]
    for copy in loads:
        copy.start()

    loads[6].wait()
    length = len_ref[y]
    loads[1].wait()
    loads[0].wait()
    passage = praw[...]
    labels = lab[pl.ds(y, 1), :]
    picked = (iota((CPAD, PTOK), 0) == labels) & (iota((CPAD, PTOK), 1) < length)
    totals = jnp.dot(
        jnp.where(picked, 1.0, 0.0).astype(BF16), passage, preferred_element_type=F32
    )
    wide = passage.astype(F32)
    masked = jnp.where(iota((PTOK, D), 0) < length, wide, wide[0:1, :])
    pas[0] = masked.astype(BF16)
    loads[2].wait()
    loads[3].wait()
    mine = jnp.where(
        (iota((CPAD, NZ * ROW), 1) == s) & (iota((CPAD, NZ * ROW), 0) == NCLUS), 1.0, 0.0
    ).astype(BF16)
    spread = jnp.where(
        iota((NCLUS, D), 0) == iota((NCLUS, D), 1), 1.0, 0.0
    ).astype(BF16)
    table = lax.dot_general(
        idf[...].astype(F32).astype(BF16), spread, (((0,), (0,)), ((), ())),
        preferred_element_type=F32,
    ).astype(BF16)
    tot[0:TROWS] = (totals + jnp.dot(mine, table, preferred_element_type=F32))[:TROWS]
    back[...] = jnp.zeros_like(back)

    pl.semaphore_wait(barrier, len(near))

    def arrive(ref, sem):
        remote(ref, ref, sem, sem, device(dc=1)).wait_recv()

    def leave(ref, sem):
        remote(ref, ref, sem, sem, device(dc=1)).wait_send()

    for dz in (2, -2):
        pl.semaphore_signal(near_sem, inc=1, device_id=device(dz=dz), device_id_type=MESH)

    def place(slot):
        return PLACES.index(slot)

    def pass_recv(slot):
        at = place(slot)
        return relay_recv.at[at] if at < HELD else rest_recv.at[at // LAST]

    def relay(entry):
        source, hops = entry
        if source:
            arrive(pas.at[place(source)], pass_recv(source))
        for dz, slot in hops:
            remote(
                pas.at[place(source)], pas.at[place(slot)],
                pas_send, pass_recv(slot), device(dz=dz),
            ).start()

    for dy in (2, 1, 3):
        pl.semaphore_signal(plane_sem, inc=1, device_id=device(dy=dy), device_id_type=MESH)

    def rows_of(slot, count=1):
        return pl.ds(slot * TROWS, count * TROWS)

    def tot_send_to(dy, dx, dc):
        slot = dy * ROW + dx * NC + dc
        remote(
            tot.at[rows_of(0)], tot.at[rows_of(slot)], tot_send, tot_recv,
            device(dy=dy, dx=dx, dc=dc),
        ).start()

    for dx, dc in row_steps:
        tot_send_to(0, dx, dc)
    for dy in (2, 1, 3):
        tot_send_to(dy, 0, 0)
    relay(RELAYS[0])
    pl.semaphore_wait(plane_sem, 3)
    for dy, dx, dc in OFFSETS:
        if dy and (dx or dc):
            tot_send_to(dy, dx, dc)
    loads[4].wait()
    loads[5].wait()
    turn = lax.rem(iota((NZ, NZ * ROW), 0) + z, NZ) * ROW + (x * NC + core)
    pick = jnp.where(iota((NZ, NZ * ROW), 1) == turn, 1.0, 0.0).astype(F32)
    ids = lax.dot_general(
        pick, fb[...].astype(F32), NT,
        precision=lax.Precision.HIGHEST, preferred_element_type=F32,
    )
    slots = iota((NZ, PLANE), 1)
    slot_y = lax.rem(y + NY - lax.div(slots, ROW), NY)
    slot_x = lax.rem(x + NX - lax.rem(lax.div(slots, NC), NX), NX)
    slot_c = lax.rem(core + lax.rem(slots, NC), 2)
    slot_id = (z * PLANE + slot_x * (NC * NY) + slot_c * NY + slot_y).astype(F32)
    counts = jnp.zeros((NZ, PLANE), F32)
    for k in range(FB):
        counts += jnp.where(jnp.abs(slot_id - ids[:, k : k + 1]) < 0.5, 1.0, 0.0)
    up = jnp.where(tenth(iota((EXP, NZ), 0)) == iota((EXP, NZ), 1), 1.0, 0.0).astype(BF16)
    wide_shape = (PLANE, PLANE * TROWS)
    over = jnp.where(eleventh(iota(wide_shape, 1)) == iota(wide_shape, 0), 1.0, 0.0).astype(BF16)
    tall = jnp.dot(up, counts.astype(BF16), preferred_element_type=F32).astype(BF16)
    counts = jnp.dot(tall, over, preferred_element_type=F32)
    to, at = iota((EXP, PLANE * TROWS), 0), iota((EXP, PLANE * TROWS), 1)
    same = to - NCLUS * tenth(to) == at - TROWS * eleventh(at)
    mix[...] = jnp.where(same, counts, 0.0).astype(BF16)

    for dx, dc in row_steps:
        slot = dx * NC + dc
        remote(
            qbuf.at[0], qbuf.at[slot], query_send, row_query_recv, device(dx=dx, dc=dc)
        ).start()
    pl.semaphore_wait(near_sem, 2)
    for dz in (4, -4):
        pl.semaphore_signal(far_sem, inc=1, device_id=device(dz=dz), device_id_type=MESH)
    for entry in RELAYS[1:LATE_RELAYS]:
        relay(entry)
    arrive(tot.at[rows_of(1, PLANE - 1)], tot_recv)

    counts = mix[...]
    summed = None
    for piece in split3(tot[...]):
        term = jnp.dot(counts, piece, preferred_element_type=F32)
        summed = term if summed is None else summed + term
    for dz in range(NZ):
        part[dz, 0:NCLUS] = summed[dz * NCLUS : (dz + 1) * NCLUS]
    pl.semaphore_wait(far_sem, 2)
    def sum_send(k):
        target = k + lax.div(k + NZ - z, NZ)
        dz = lax.rem(target + NZ - z, NZ)
        remote(
            part.at[dz, pl.ds(0, NCLUS)], rs.at[dz, pl.ds(0, NCLUS)],
            rs_send, rs_recv, device(dz=dz),
        ).start()

    for k in range(FIRST):
        sum_send(k)
    arrive(qbuf.at[pl.ds(1, ROW - 1)], row_query_recv)
    for dy in (2, 1, 3):
        remote(
            qbuf.at[pl.ds(0, ROW)], qbuf.at[pl.ds(dy * ROW, ROW)],
            query_send, col_query_recv, device(dy=dy),
        ).start()

    lanes = iota((D, EROWS), 1)
    spread = jnp.where(lanes - NCLUS * tenth(lanes) == iota((D, EROWS), 0), 1.0, 0.0).astype(BF16)
    idf_rows = tot[pl.ds(NCLUS, PLANE, stride=TROWS), :].astype(BF16)
    idf_rows = jnp.dot(idf_rows, spread, preferred_element_type=F32)
    owner = tenth(iota((PLANE, EROWS), 1))
    exp_weight = jnp.where(owner == iota((PLANE, EROWS), 0), idf_rows, 0.0).astype(BF16)
    query_weight = jnp.where(
        lax.div(iota((PLANE, QROWS), 1), QTOK) == iota((PLANE, QROWS), 0), 1.0, 0.0
    ).astype(BF16)

    for entry in RELAYS[LATE_RELAYS : LATE_RELAYS + 2]:
        relay(entry)
    for k in range(FIRST, NZ - 1):
        sum_send(k)
    for entry in RELAYS[LATE_RELAYS + 2 :]:
        relay(entry)

    arrive(rs.at[pl.ds(1, NZ - 1), pl.ds(0, NCLUS)], rs_recv)
    rows = part[0, 0:NCLUS]
    for dz in range(1, NZ):
        rows += rs[dz, 0:NCLUS]
    factor = lax.rsqrt(jnp.mean(rows * rows, axis=1, keepdims=True) + 1e-06)
    exb[0:NCLUS] = (rows * factor).astype(BF16)
    for dy, dx, dc in OFFSETS:
        slot = dy * ROW + dx * NC + dc
        remote(
            exb.at[pl.ds(0, NCLUS)], exb.at[pl.ds(slot * NCLUS, NCLUS)], exp_send, exp_recv,
            device(dy=dy, dx=dx, dc=dc),
        ).start()

    arrive(qbuf.at[pl.ds(ROW, PLANE - ROW)], col_query_recv)
    def score(vectors, out, at, first, last):
        for n in range(first, last, GROUP):
            stop = min(n + GROUP, last)
            tokens = pas[n:stop].reshape((stop - n) * PTOK, D)
            scores = lax.dot_general(tokens, vectors, NT, preferred_element_type=F32)
            for m in range(n, stop):
                top = scores[(m - n) * PTOK : (m - n + 1) * PTOK]
                out[m : m + 1, at : at + vectors.shape[0]] = jnp.max(top, axis=0, keepdims=True)

    def plain_score(first, last):
        for tile in range(QROWS // TILE):
            vectors = qbuf[tile * ROW : (tile + 1) * ROW].reshape(TILE, D)
            score(vectors, best, tile * TILE, first, last)

    plain_score(0, HELD)
    arrive(pas.at[pl.ds(HELD, LAST - HELD)], rest_recv.at[0])
    plain_score(HELD, LAST)
    arrive(pas.at[pl.ds(LAST, NZ - LAST)], rest_recv.at[1])
    plain_score(LAST, NZ)

    def reduce(weight, values):
        hi, mid, low = split3(values)
        total = lax.dot_general(weight, hi, NT, preferred_element_type=F32)
        total += lax.dot_general(weight, mid, NT, preferred_element_type=F32)
        return total + lax.dot_general(weight, low, NT, preferred_element_type=F32)

    plain = reduce(query_weight, best[...]) * (1.0 / QTOK)
    back[:, 0:NZ] = plain

    ids = cand[...]
    cand_y = lax.rem(ids, NY)
    cand_c = lax.rem(lax.div(ids, NY), NC)
    cand_x = lax.rem(lax.div(ids, NY * NC), NX)
    cand_z = lax.div(ids, PLANE)
    cand_slot = (
        lax.rem(cand_y + NY - y, NY) * ROW
        + lax.rem(cand_x + NX - x, NX) * NC
        + lax.rem(cand_c + core, 2)
    )
    cand_n = lax.rem(z + NZ - cand_z, NZ)
    slot_hot = jnp.where(iota((PLANE, NCAND), 0) == cand_slot, 1.0, 0.0).astype(BF16)
    held = iota((NZ, NCAND), 0)
    slot_at = jnp.zeros((NZ, NCAND), jnp.int32)
    for at, slot in enumerate(PLACES):
        slot_at = jnp.where(held == at, slot, slot_at)
    n_hot = slot_at == cand_n

    arrive(exb.at[pl.ds(NCLUS, EROWS - NCLUS)], exp_recv)
    for at in range(0, EROWS, TILE):
        score(exb[at : min(at + TILE, EROWS)], best_exp, at, 0, NZ)
    added = reduce(exp_weight, best_exp[...]) * (1.0 / (8.0 * NCLUS))
    back[:, NZ : 2 * NZ] = plain + added

    for dy, dx, dc in OFFSETS:
        slot = dy * ROW + dx * NC + dc
        remote(
            back.at[pl.ds(slot, 1)], ret.at[pl.ds(slot, 1)], ret_send, ret_recv,
            device(dy=-dy, dx=-dx, dc=dc),
        ).start()
    ret[0:1, :] = back[0:1, :]
    others = pl.ds(1, PLANE - 1)
    leave(tot.at[rows_of(1, PLANE - 1)], tot_send)
    leave(qbuf.at[others], query_send)
    leave(pas.at[pl.ds(1, NZ - 1)], pas_send)
    leave(rs.at[pl.ds(1, NZ - 1), pl.ds(0, NCLUS)], rs_send)
    leave(exb.at[pl.ds(NCLUS, EROWS - NCLUS)], exp_send)
    arrive(ret.at[others], ret_recv)
    flat = ret[...].T[: 2 * NZ, :]
    chosen = None
    for piece in split3(flat):
        term = jnp.dot(piece, slot_hot, preferred_element_type=F32)
        chosen = term if chosen is None else chosen + term
    out_ref[0:1, :] = jnp.sum(jnp.where(n_hot, chosen[:NZ], 0.0), axis=0, keepdims=True)
    out_ref[1:2, :] = jnp.sum(jnp.where(n_hot, chosen[NZ:], 0.0), axis=0, keepdims=True)
    leave(ret.at[others], ret_send)


def local(queries, passages, labels, lengths, candidates, feedback, idf):
    dma = pltpu.SemaphoreType.DMA
    anywhere = pl.BlockSpec(memory_space=pl.ANY)
    scores = pl.pallas_call(
        kernel,
        out_shape=pltpu.VMEM((2, NCAND), F32),
        in_specs=[anywhere] * 7,
        out_specs=pl.BlockSpec(memory_space=pltpu.VMEM),
        scratch_shapes=[
            pltpu.SMEM((NY,), jnp.int32),
            pltpu.VMEM((PLANE, QTOK, D), BF16),
            pltpu.VMEM((PTOK, D), BF16),
            pltpu.VMEM((NZ, PTOK, D), BF16),
            pltpu.VMEM((NY, PTOK), jnp.int32),
            pltpu.VMEM((1, NCAND), jnp.int32),
            pltpu.VMEM((FB, NZ * ROW), jnp.int32),
            pltpu.VMEM((NCLUS, NZ * ROW), jnp.int32),
            pltpu.VMEM((PLANE * TROWS, D), F32),
            pltpu.VMEM((EXP, PLANE * TROWS), BF16),
            pltpu.VMEM((NZ, CPAD, D), F32),
            pltpu.VMEM((NZ, CPAD, D), F32),
            pltpu.VMEM((EROWS, D), BF16),
            pltpu.VMEM((NZ, QROWS), F32),
            pltpu.VMEM((NZ, EROWS), F32),
            pltpu.VMEM((PLANE, D), F32),
            pltpu.VMEM((PLANE, D), F32),
            dma((7,)),
            dma, dma,
            dma, dma, dma,
            dma, dma((HELD,)), dma((2,)),
            dma, dma,
            dma, dma,
            dma, dma,
            pltpu.SemaphoreType.REGULAR,
            pltpu.SemaphoreType.REGULAR,
            pltpu.SemaphoreType.REGULAR,
        ],
        compiler_params=pltpu.CompilerParams(collective_id=0, has_side_effects=True),
    )(queries, passages, labels, lengths, candidates, feedback.T, idf.T)
    return scores[0:1], scores[1:2]


def solution(mesh):
    return jax.shard_map(
        local,
        mesh=mesh,
        in_specs=(
            P(("rep", "shard"), None, None),
            P(("shard", "rep"), None, None),
            P("shard", None),
            P("shard"),
            P(("rep", "shard"), None),
            P("rep", None),
            P("rep", None),
        ),
        out_specs=(P(("rep", "shard"), None), P(("rep", "shard"), None)),
        check_vma=False,
    )
```
